32 devices in a mesh: dp: 16 (over z, x, core), vol: 2 (over y).
Axes of the slice: x: 2, y: 2, z: 4, core: 2. Of those that a mesh axis runs over, the one named last changes fastest.
Arguments:
- images: float32 [32, 128, 128], P(('dp', 'vol')), may hold values from -6 to 6
- contrast: bfloat16 [32, 128, 128], P(('dp', 'vol')), may hold values from -1 to 1
- volume: bfloat16 [256, 256, 256], P('vol'), may hold values from -6 to 6
- line_index: int32 [32, 4, 128], P('dp'), may hold values from 0 to 65278, as said below
- patch_weight: bfloat16 [64, 1024], replicated, may hold values from -0.75 to 0.75
- position: bfloat16 [256, 1024], replicated, may hold values from -3 to 3
- norm_gain: float32 [1024], replicated, may hold values from 0.1 to 1.9
- project_in: bfloat16 [1024, 1536], P('dp'), may hold values from -0.1875 to 0.1875
- project_out: bfloat16 [1024, 512], P('dp'), may hold values from -0.25 to 0.25
- head_weight: float32 [1024, 4], replicated, may hold values from -1.8 to 1.8
Outputs:
- errors: float32 [32, 4], P(('dp', 'vol'))
- in_gradient: float32 [1024, 1536], P('dp')
- out_gradient: float32 [1024, 512], P('dp')
- head_gradient: float32 [1024, 4], replicated
The draws below stay inside these ranges and needn't reach their ends.
Inputs may be any that keep to these rules, and one draw needn't show every extreme that they name: line_index[i, k, r] = z * 256 + y names the plane z and row y of the volume that row r of hypothesis k of image i samples; z and y lie within 0 and 254.
All inputs are finite; a program needn't handle non-finite values.
Results may differ from the reference program's by a relative error of at most 0.038.
Values may be sent and summed in bfloat16 or wider, within the bound.
A program may use at most 64 MiB of HBM per device.

```python
import jax
import jax.numpy as jnp
from jax import lax

D = 1024
HEADS = 8
HEAD_DIM = 64
HD = 512
PIX = 128
PATCH = 8
PATCHES = 256
VOX = 256
K = 4
IMAGES = 32


def draw_line_index(key, part):
    first, second = jax.random.split(jax.random.fold_in(key, 7))
    tilt = jax.random.randint(first, (IMAGES, K), -14, 17)
    turn = jax.random.randint(second, (IMAGES, K), 0, 17)
    tilt = tilt.at[0, 0].set(16)
    turn = turn.at[0, 0].set(16)
    offset = 2 * (jnp.arange(PIX, dtype=jnp.int32) - PIX // 2)
    plane = VOX // 2 + offset[None, None, :] * tilt[:, :, None] // 16
    row = VOX // 2 + offset[None, None, :] * turn[:, :, None] // 16
    return (plane * VOX + row).astype(jnp.int32)


def steps_of(rng, shape, cuts, smallest, top_value):
    def one(dim, blocks):
        heights = jax.random.uniform(jax.random.fold_in(jax.random.fold_in(rng, 6), dim), (blocks,), jnp.float32, smallest / len(cuts), top_value / len(cuts))
        return jnp.repeat(jnp.exp(heights), shape[dim] // blocks).reshape((-1,) + (1,) * (len(shape) - dim - 1))

    gain = one(*cuts[0])
    for cut in cuts[1:]:
        gain = gain * one(*cut)
    return gain


def centred(rng, shape, scale, most, cuts=(), kind=jnp.bfloat16):
    entries = jax.random.normal(rng, shape, jnp.float32) * scale
    if len(cuts) > 0:
        entries = steps_of(rng, shape, cuts, -0.22, 0.18) * entries
    return jnp.clip(entries, min=-most, max=most).astype(kind)


def setup_inputs(seed: int = 0) -> dict:
    seeds = jax.random.split(jax.random.key(seed), 11)
    images = centred(seeds[0], (IMAGES, PIX, PIX), 1.0, 6.0, ((0, 32),), jnp.float32)
    contrast = jnp.clip(jax.random.uniform(seeds[1], (IMAGES, PIX, PIX), jnp.float32, -1.0, 1.0) * steps_of(seeds[1], (IMAGES, PIX, PIX), ((0, 32),), -0.4, 0.0), -1.0, 1.0).astype(jnp.bfloat16)
    volume = centred(seeds[2], (VOX, VOX, VOX), 1.0, 6.0, ((0, 2),))
    line_index = draw_line_index(jax.random.fold_in(seeds[10], 71), 0)
    patch_weight = centred(seeds[4], (PATCH * PATCH, D), (PATCH * PATCH) ** -0.5, 0.75)
    position = centred(seeds[5], (PATCHES, D), 0.5, 3.0)
    norm_gain = jnp.clip(1.0 + 0.18 * jax.random.normal(seeds[6], (D,), jnp.float32), 0.1, 1.9)
    project_in = centred(seeds[7], (D, 3 * HD), D ** -0.5, 0.1875, ((0, 16),))
    project_out = centred(seeds[8], (D, HD), HD ** -0.5, 0.25, ((0, 16),))
    head_weight = centred(seeds[9], (D, K), 0.3, 1.8, (), jnp.float32)
    return {"images": images, "contrast": contrast, "volume": volume, "line_index": line_index, "patch_weight": patch_weight, "position": position, "norm_gain": norm_gain, "project_in": project_in, "project_out": project_out, "head_weight": head_weight}


EPSILON = 1e-05

def embed_images(images, patch_weight, position):
    count = images.shape[0]
    grid = PIX // PATCH
    pieces = images.reshape(count, grid, PATCH, grid, PATCH).transpose(0, 1, 3, 2, 4)
    pieces = pieces.reshape(count * grid * grid, PATCH * PATCH).astype(jnp.bfloat16)
    mixed = jnp.dot(pieces, patch_weight, preferred_element_type=jnp.float32)
    mixed = mixed.reshape(count, grid * grid, -1) + position.astype(jnp.float32)[None]
    return mixed.reshape(count * grid * grid, -1).astype(jnp.bfloat16)

def normalize(embedded, norm_gain):
    values = embedded.astype(jnp.float32)
    center = values - lax.optimization_barrier(jnp.mean(values, axis=1, keepdims=True))
    scale = lax.rsqrt(lax.optimization_barrier(jnp.mean(center * center, axis=1, keepdims=True)) + EPSILON)
    return (center * scale * norm_gain[None, :]).astype(jnp.bfloat16)

def attend(triple):
    count = triple.shape[0] // PATCHES
    parts = triple.reshape(count, PATCHES, 3, HEADS, HEAD_DIM).astype(jnp.float32)
    query = parts[:, :, 0]
    keys = parts[:, :, 1]
    values = parts[:, :, 2]
    scores = jnp.einsum('bqhd,bkhd->bhqk', query, keys) * HEAD_DIM ** (-0.5)
    raised = jnp.exp(scores)
    weights = (raised / lax.optimization_barrier(jnp.sum(raised, axis=-1, keepdims=True))).astype(jnp.bfloat16)
    mixed = jnp.einsum('bhqk,bkhd->bqhd', weights.astype(jnp.float32), values)
    return mixed.reshape(count * PATCHES, HEADS * HEAD_DIM).astype(jnp.bfloat16)

def spectrum_of(images):
    transform = jnp.fft.fftshift(jnp.fft.fft2(images), axes=(1, 2))
    return (jnp.real(transform) - jnp.imag(transform)) / PIX

def reference(images, contrast, volume, line_index, patch_weight, position, norm_gain, project_in, project_out, head_weight):
    table = volume.reshape(VOX * VOX, VOX)
    block = 16
    blocks = IMAGES // block
    image_blocks = images.reshape(blocks, block, PIX, PIX)
    contrast_blocks = contrast.reshape(blocks, block, PIX, PIX)
    line_blocks = line_index.reshape(blocks, block, K, PIX)

    def step(carry, inputs):
        image_part, contrast_part, line_part = inputs
        picked = jnp.take(table, line_part.reshape(-1), axis=0)[:, ::2]
        slices = picked.astype(jnp.float32).reshape(block, K, PIX, PIX)
        spectrum = spectrum_of(image_part)
        misfit = contrast_part.astype(jnp.float32)[:, None] * slices - spectrum[:, None]
        errors = lax.optimization_barrier(jnp.mean(misfit * misfit, axis=(2, 3)))
        embedded = embed_images(image_part, patch_weight, position)
        normed = normalize(embedded, norm_gain)
        triple = jnp.dot(normed, project_in, preferred_element_type=jnp.float32).astype(jnp.bfloat16)
        attended = attend(triple)
        branch = jnp.dot(attended, project_out.T, preferred_element_type=jnp.float32)
        layer_out = embedded.astype(jnp.float32) + branch
        pooled = lax.optimization_barrier(jnp.mean(layer_out.reshape(block, PATCHES, D), axis=1))
        logits = jnp.dot(pooled, head_weight, precision=lax.Precision.HIGHEST)
        raised = jnp.exp(logits)
        chances = raised / lax.optimization_barrier(jnp.sum(raised, axis=1, keepdims=True))
        expected = lax.optimization_barrier(jnp.sum(chances * errors, axis=1, keepdims=True))
        logit_slope = chances * (errors - expected)
        head_term = jnp.dot(pooled.T, logit_slope, precision=lax.Precision.HIGHEST)
        pooled_slope = jnp.dot(logit_slope, head_weight.T, precision=lax.Precision.HIGHEST) / PATCHES
        layer_slope = jnp.broadcast_to(pooled_slope[:, None, :], (block, PATCHES, D)).reshape(block * PATCHES, D).astype(jnp.bfloat16)
        out_term = jnp.dot(layer_slope.T, attended, preferred_element_type=jnp.float32)
        attended_slope = jnp.dot(layer_slope, project_out, preferred_element_type=jnp.float32).astype(jnp.bfloat16)
        triple_slope = jax.vjp(attend, triple)[1](attended_slope)[0]
        in_term = jnp.dot(normed.T, triple_slope, preferred_element_type=jnp.float32)
        in_sum, out_sum, head_sum = carry
        return ((in_sum + in_term, out_sum + out_term, head_sum + head_term), errors)
    start = (jnp.zeros((D, 3 * HD), jnp.float32), jnp.zeros((D, HD), jnp.float32), jnp.zeros((D, K), jnp.float32))
    totals, errors = lax.scan(step, start, (image_blocks, contrast_blocks, line_blocks))
    return (errors.reshape(IMAGES, K), totals[0], totals[1], totals[2])
```

```python
import functools
import math

import jax
import jax.numpy as jnp
import numpy as np
from jax import lax
from jax.experimental import pallas as pl
from jax.experimental.pallas import tpu as pltpu
from jax.sharding import PartitionSpec as P

HEADS = 8
HEAD_DIM = 64
PIX = 128
PATCH = 8
PATCHES = 256
K = 4
EPSILON = 1e-05
F32 = jnp.float32
BF16 = jnp.bfloat16
HIGHEST = lax.Precision.HIGHEST
FIRST = (((0,), (0,)), ((), ()))
LAST = (((1,), (1,)), ((), ()))
MESH = pl.DeviceIdType.MESH


def step(
    dps,
    vols,
    picked,
    patches,
    pieces,
    image,
    contrast,
    patch_weight,
    position,
    gain,
    head_t,
    head_own,
    waves,
    sel,
    errors_out,
    in_out,
    out_out,
    head_out,
    lines,
    patch_buf,
    weight,
    normed,
    attention,
    triple,
    column,
    mean_emb,
    mean_att,
    small_send,
    small_recv,
    total,
    grad_send,
    tile_send,
    grad_recv,
    tile_recv,
    head_send,
    line_sems,
    patch_sems,
    weight_sems,
    small_sems,
    grad_sems,
    tile_sems,
    head_sems,
    local_sems,
):
    dp = lax.axis_index("dp")
    vol = lax.axis_index("vol")
    count = dps * vols
    me = dp * vols + vol
    head = dp % HEADS
    base = dp - head
    rows = weight.shape[1]
    width = gain.shape[1]

    def copy(src, dst, sems, slot_send, slot_recv, to_dp, to_vol):
        return pltpu.make_async_remote_copy(
            src_ref=src,
            dst_ref=dst,
            send_sem=sems.at[0, slot_send],
            recv_sem=sems.at[1, slot_recv],
            device_id=(to_dp, to_vol),
            device_id_type=MESH,
        )

    barrier = pltpu.get_barrier_semaphore()

    def greet(k, c):
        other = (me + k) % count
        pl.semaphore_signal(
            barrier, inc=1, device_id=(other // vols, other % vols), device_id_type=MESH
        )
        return c

    lax.fori_loop(1, count, greet, 0)
    pl.semaphore_wait(barrier, count - 1)

    def patch_copy(k, slot):
        to = base + (head + k) % HEADS
        return copy(patches, patch_buf.at[slot], patch_sems, k, slot, to, vol)

    def weight_copy(k, slot):
        to = (dp + k) % dps
        return copy(pieces.at[to % HEADS], weight.at[slot], weight_sems, k, slot, to, vol)

    def line_copy(k, slot):
        to = (vol + k) % vols
        return copy(picked.at[to], lines.at[slot], line_sems, k, slot, dp, to)

    def each(first, last, body):
        def run(k, c):
            body(k)
            return c

        lax.fori_loop(first, last, run, 0)

    each(1, HEADS, lambda k: patch_copy(k, head).start())
    each(1, dps, lambda k: weight_copy(k, dp).start())
    each(1, vols, lambda k: line_copy(k, vol).start())
    own = [
        pltpu.make_async_copy(patches, patch_buf.at[head], local_sems.at[0]),
        pltpu.make_async_copy(pieces.at[head], weight.at[dp], local_sems.at[1]),
        pltpu.make_async_copy(picked.at[vol], lines.at[vol], local_sems.at[2]),
    ]
    for one in own:
        one.start()

    cosine = waves[0]
    sine = waves[1]
    pixels = image[0]
    first_cos = jnp.dot(cosine, pixels, precision=HIGHEST, preferred_element_type=F32)
    first_sin = jnp.dot(sine, pixels, precision=HIGHEST, preferred_element_type=F32)
    spectrum = jnp.dot(first_cos, waves[2], precision=HIGHEST, preferred_element_type=F32)
    spectrum = spectrum + jnp.dot(
        first_sin, waves[3], precision=HIGHEST, preferred_element_type=F32
    )
    spectrum = spectrum / PIX

    own[0].wait()

    def embed(k, c):
        j = (head + k) % HEADS

        @pl.when(k > 0)
        def _():
            patch_copy(HEADS - k, j).wait_recv()

        pair = patch_buf[j]
        sums = jnp.zeros((1, width), F32)
        for half in range(2):
            part = slice(half * 128, half * 128 + 128)
            values = jnp.dot(
                pair[:, half * 64 : half * 64 + 64],
                patch_weight[...],
                preferred_element_type=F32,
            )
            values = (values + position[part].astype(F32)).astype(BF16).astype(F32)
            sums = sums + jnp.sum(values, axis=0, keepdims=True)
            center = values - jnp.mean(values, axis=1, keepdims=True)
            scale = lax.rsqrt(jnp.mean(center * center, axis=1, keepdims=True) + EPSILON)
            normed[j, part, :] = (center * scale * gain[...]).astype(BF16)
        mean_emb[pl.ds(j, 1), :] = sums / PATCHES
        return c

    lax.fori_loop(0, HEADS, embed, 0)

    own[1].wait()
    each(1, dps, lambda k: weight_copy(k, (dp + dps - k) % dps).wait_recv())

    out_w = weight[:, :, 192:256].reshape(width, HEAD_DIM).astype(F32)
    mixed = jnp.dot(head_t[...], out_w, precision=HIGHEST, preferred_element_type=F32)

    def forward(j, c):
        whole = weight[...].reshape(width, 256)
        t = jnp.dot(normed[j], whole, preferred_element_type=F32).astype(BF16)
        triple[j] = t
        scores = (
            lax.dot_general(t[:, 64:128], t[:, 0:64], LAST, preferred_element_type=F32)
            * HEAD_DIM ** (-0.5)
        )
        raised = jnp.exp(scores)
        chosen = (raised / jnp.sum(raised, axis=0, keepdims=True)).astype(BF16)
        attention[j] = chosen
        col = jnp.sum(chosen.astype(F32), axis=1, keepdims=True)
        column[j] = col
        mean_att[pl.ds(j, 1), :] = (
            jnp.sum(col * t[:, 128:192].astype(F32), axis=0, keepdims=True) / PATCHES
        )
        return c

    lax.fori_loop(0, HEADS, forward, 0)

    own[2].wait()
    each(1, vols, lambda k: line_copy(k, (vol + vols - k) % vols).wait_recv())
    rendered = lines[0].astype(F32)
    for other in range(1, vols):
        rendered = rendered + lines[other].astype(F32)
    slices = jnp.dot(rendered.astype(BF16), sel[...], preferred_element_type=F32)
    lane = lax.broadcasted_iota(jnp.int32, (HEADS, 128), 1)
    row = lax.broadcasted_iota(jnp.int32, (HEADS, 128), 0)
    filt = contrast[0].astype(F32)
    misfits = jnp.zeros((HEADS, 128), F32)
    for k in range(K):
        misfit = filt * slices[k * PIX : (k + 1) * PIX] - spectrum
        value = jnp.sum(jnp.sum(misfit * misfit, axis=0, keepdims=True), axis=1, keepdims=True)
        misfits = jnp.where(lane == k, value / (PIX * PIX), misfits)
    errors_out[...] = misfits
    mine = row == head
    own_emb = jnp.where(
        lax.broadcasted_iota(jnp.int32, (HEADS, width), 0) == head, mean_emb[...], 0.0
    )
    logit = lax.dot_general(
        own_emb, head_t[...], LAST, precision=HIGHEST, preferred_element_type=F32
    )
    logit = logit + lax.dot_general(
        mean_att[...], mixed, LAST, precision=HIGHEST, preferred_element_type=F32
    )
    small_send[0:8, :] = jnp.concatenate([logit, jnp.zeros((HEADS, 120), F32)], axis=1)
    small_send[8:16, :] = jnp.where(mine, misfits, 0.0)

    def small_copy(k, slot):
        to = base + (head + k) % HEADS
        return copy(small_send, small_recv.at[slot], small_sems, k, slot, to, vol)

    each(1, HEADS, lambda k: small_copy(k, head).start())
    small_recv[head] = small_send[...]
    each(1, HEADS, lambda k: small_copy(k, (head + HEADS - k) % HEADS).wait_recv())
    summed = jnp.sum(small_recv[...], axis=0)
    misfits = summed[8:16]
    raised = jnp.where(lane < K, jnp.exp(summed[0:8]), 0.0)
    chances = raised / jnp.sum(raised, axis=1, keepdims=True)
    expected = jnp.sum(chances * misfits, axis=1, keepdims=True)
    slope = chances * (misfits - expected)
    pulled = jnp.zeros((HEADS, HEAD_DIM), F32)
    for k in range(K):
        pulled = pulled + slope[:, k : k + 1] * mixed[k : k + 1, :]
    pulled = pulled / PATCHES
    small_send_slope = slope
    total[...] = jnp.zeros(total.shape, F32)

    for j in range(HEADS):
        t = triple[j]
        chosen = attention[j].astype(F32)
        up = jnp.sum(t[:, 128:192].astype(F32) * pulled[j : j + 1, :], axis=1, keepdims=True)
        center = jnp.sum(chosen * up, axis=0, keepdims=True)
        inner = (chosen * (up - center) * HEAD_DIM ** (-0.5)).astype(BF16)
        key_slope = jnp.dot(inner, t[:, 0:64], preferred_element_type=F32)
        query_slope = lax.dot_general(inner, t[:, 64:128], FIRST, preferred_element_type=F32)
        spread = column[j] * small_send_slope[j : j + 1, :]
        terms = jnp.concatenate([query_slope, key_slope, spread], axis=1).astype(BF16)
        total[...] += lax.dot_general(terms, normed[j], FIRST, preferred_element_type=F32)

    outer = lax.dot_general(
        slope, mean_att[...], FIRST, precision=HIGHEST, preferred_element_type=F32
    )[0:8]
    pooled_t = lax.dot_general(
        jnp.where(mine, slope, 0.0),
        own_emb,
        FIRST,
        precision=HIGHEST,
        preferred_element_type=F32,
    )[0:8]
    pooled_t = pooled_t + lax.dot_general(
        outer, out_w, LAST, precision=HIGHEST, preferred_element_type=F32
    )
    value_t = total[128:136, :]
    for d in range(dps):
        part = slice(d * rows, (d + 1) * rows)
        grad_send[d] = total[0:128, part].T.astype(BF16)
        fill = [jnp.zeros((HEADS, 64 - rows), F32)] if rows < 64 else []
        top = jnp.concatenate([value_t[:, part]] + fill + [outer], axis=1)
        low = jnp.concatenate([mixed] + [pooled_t[:, part]] + fill, axis=1)
        tile_send[d] = jnp.where(row < 4, top, pltpu.roll(low, 4, 0))

    def grad_copy(k, slot):
        to = (me + k) % count
        return copy(
            grad_send.at[to // vols], grad_recv.at[slot], grad_sems, k, slot, to // vols, to % vols
        )

    def tile_copy(k, slot):
        to = (me + k) % count
        return copy(
            tile_send.at[to // vols], tile_recv.at[slot], tile_sems, k, slot, to // vols, to % vols
        )

    each(1, count, lambda k: tile_copy(k, me).start())
    each(1, count, lambda k: grad_copy(k, me).start())
    grad_recv[me] = grad_send[dp]
    tile_recv[me] = tile_send[dp]
    each(1, count, lambda k: tile_copy(k, (me + count - k) % count).wait_recv())

    pooled_sum = jnp.sum(tile_recv[...], axis=0)
    head_send[...] = pooled_sum

    def head_copy(k, slot):
        to = (dp + k) % dps
        return copy(head_send, head_out.at[slot], head_sems, k, slot, to, vol)

    each(1, dps, lambda k: head_copy(k, dp).start())
    head_out[dp] = pooled_sum

    for h in range(HEADS):
        senders = [
            (d * vols + v) for d in range(h, dps, HEADS) for v in range(vols)
        ]
        tile = tile_recv[senders[0]]
        mixed_h = jnp.where(row < 4, pltpu.roll(tile, 4, 0), 0.0)[:, 0:64]
        for s in senders[1:]:
            tile = tile + tile_recv[s]
        tile = jnp.where(row < 4, tile, 0.0)
        lanes = slice(h * 64, h * 64 + 64)
        in_out[:, 1024 + h * 64 : 1088 + h * 64] = (
            lax.dot_general(
                tile[:, 0:rows], mixed_h, FIRST, precision=HIGHEST, preferred_element_type=F32
            )
            / PATCHES
        )
        out_out[:, lanes] = lax.dot_general(
            head_own[...], tile[:, 64:128], FIRST, precision=HIGHEST, preferred_element_type=F32
        )
    each(1, count, lambda k: grad_copy(k, (me + count - k) % count).wait_recv())
    for h in range(HEADS):
        senders = [
            (d * vols + v) for d in range(h, dps, HEADS) for v in range(vols)
        ]
        both = grad_recv[senders[0]].astype(F32)
        for s in senders[1:]:
            both = both + grad_recv[s].astype(F32)
        in_out[:, h * 64 : h * 64 + 64] = both[:, 0:64]
        in_out[:, 512 + h * 64 : 576 + h * 64] = both[:, 64:128]
    each(1, dps, lambda k: head_copy(k, (dp + dps - k) % dps).wait_recv())

    each(1, HEADS, lambda k: patch_copy(k, head).wait_send())
    each(1, dps, lambda k: weight_copy(k, dp).wait_send())
    each(1, vols, lambda k: line_copy(k, vol).wait_send())
    each(1, HEADS, lambda k: small_copy(k, head).wait_send())
    each(1, count, lambda k: tile_copy(k, me).wait_send())
    each(1, count, lambda k: grad_copy(k, me).wait_send())
    each(1, dps, lambda k: head_copy(k, dp).wait_send())


def constants():
    freq = np.arange(PIX) - PIX // 2
    phase = (freq[:, None] * np.arange(PIX)[None, :] % PIX) * (2.0 * math.pi / PIX)
    cosine, sine = np.cos(phase), np.sin(phase)
    waves = np.stack([cosine, sine, (cosine + sine).T, (cosine - sine).T]).astype(np.float32)
    sel = np.zeros((2 * PIX, PIX), np.float32)
    sel[2 * np.arange(PIX), np.arange(PIX)] = 1.0
    return waves, sel


def local(
    dps,
    vols,
    images,
    contrast,
    volume,
    line_index,
    patch_weight,
    position,
    norm_gain,
    project_in,
    project_out,
    head_weight,
):
    width = norm_gain.shape[0]
    rows = project_in.shape[0]
    count = dps * vols
    waves, sel = constants()
    slab, side, _ = volume.shape
    plane = line_index // side - lax.axis_index("vol") * slab
    inside = (plane >= 0) & (plane < slab)
    spot = jnp.clip(plane, 0, slab - 1) * side + line_index % side
    picked = jnp.take(volume.reshape(slab * side, side), spot.reshape(-1), axis=0)
    picked = jnp.where(inside.reshape(-1, 1), picked, jnp.zeros((), BF16))
    picked = picked.reshape(vols, K * PIX, side)

    grid = PIX // PATCH
    patches = images[0].astype(BF16).reshape(2, grid // 2, PATCH, grid, PATCH)
    patches = patches.transpose(1, 3, 0, 2, 4).reshape(PATCHES // 2, 2 * PATCH * PATCH)
    parts = project_in.reshape(rows, 3, HEADS, HEAD_DIM).transpose(2, 0, 1, 3)
    pieces = jnp.concatenate(
        [parts, project_out.reshape(rows, HEADS, 1, HEAD_DIM).transpose(1, 0, 2, 3)], axis=2
    ).reshape(HEADS, rows, 4 * HEAD_DIM)
    head_t = jnp.pad(head_weight.T, ((0, 4), (0, 0)))
    head_own = lax.dynamic_slice(head_t, (0, lax.axis_index("dp") * rows), (8, rows))

    vmem = pl.BlockSpec(memory_space=pltpu.VMEM)
    errors, in_grad, out_grad, head_grad = pl.pallas_call(
        functools.partial(step, dps, vols),
        out_shape=(
            jax.ShapeDtypeStruct((8, 128), F32),
            jax.ShapeDtypeStruct((rows, 3 * HEADS * HEAD_DIM), F32),
            jax.ShapeDtypeStruct((rows, HEADS * HEAD_DIM), F32),
            jax.ShapeDtypeStruct((dps, 8, 128), F32),
        ),
        in_specs=[vmem] * 12,
        out_specs=(vmem,) * 4,
        scratch_shapes=[
            pltpu.VMEM((vols, K * PIX, side), BF16),
            pltpu.VMEM((HEADS, PATCHES // 2, 128), BF16),
            pltpu.VMEM((dps, rows, 256), BF16),
            pltpu.VMEM((HEADS, PATCHES, width), BF16),
            pltpu.VMEM((HEADS, PATCHES, PATCHES), BF16),
            pltpu.VMEM((HEADS, PATCHES, 256), BF16),
            pltpu.VMEM((HEADS, PATCHES, 1), F32),
            pltpu.VMEM((HEADS, width), F32),
            pltpu.VMEM((HEADS, HEAD_DIM), F32),
            pltpu.VMEM((16, 128), F32),
            pltpu.VMEM((HEADS, 16, 128), F32),
            pltpu.VMEM((256, width), F32),
            pltpu.VMEM((dps, rows, 128), BF16),
            pltpu.VMEM((dps, 8, 128), F32),
            pltpu.VMEM((count, rows, 128), BF16),
            pltpu.VMEM((count, 8, 128), F32),
            pltpu.VMEM((8, 128), F32),
            pltpu.SemaphoreType.DMA((2, vols)),
            pltpu.SemaphoreType.DMA((2, HEADS)),
            pltpu.SemaphoreType.DMA((2, dps)),
            pltpu.SemaphoreType.DMA((2, HEADS)),
            pltpu.SemaphoreType.DMA((2, count)),
            pltpu.SemaphoreType.DMA((2, count)),
            pltpu.SemaphoreType.DMA((2, dps)),
            pltpu.SemaphoreType.DMA((3,)),
        ],
        compiler_params=pltpu.CompilerParams(
            collective_id=0, has_side_effects=True, vmem_limit_bytes=56 * 1024 * 1024
        ),
        name="pose_step",
    )(
        picked,
        patches,
        pieces,
        images,
        contrast,
        patch_weight,
        position,
        norm_gain.reshape(1, width),
        head_t,
        head_own,
        jnp.asarray(waves),
        jnp.asarray(sel, BF16),
    )
    head_grad = head_grad[:, 4:8, 64 : 64 + rows].transpose(0, 2, 1).reshape(width, 4)
    return errors[0:1, 0:K], in_grad, out_grad, head_grad


def solution(mesh):
    placed = (
        P(("dp", "vol"), None, None),
        P(("dp", "vol"), None, None),
        P("vol", None, None),
        P("dp", None, None),
        P(),
        P(),
        P(),
        P("dp", None),
        P("dp", None),
        P(),
    )
    return jax.shard_map(
        functools.partial(local, mesh.shape["dp"], mesh.shape["vol"]),
        mesh=mesh,
        in_specs=placed,
        out_specs=(P(("dp", "vol"), None), P("dp", None), P("dp", None), P()),
        check_vma=False,
    )
```

```python
import functools
import math

import jax
import jax.numpy as jnp
import numpy as np
from jax import lax
from jax.experimental import pallas as pl
from jax.experimental.pallas import tpu as pltpu
from jax.sharding import PartitionSpec as P

HEADS = 8
HEAD_DIM = 64
PIX = 128
PATCH = 8
PATCHES = 256
K = 4
EPSILON = 1e-05
F32 = jnp.float32
BF16 = jnp.bfloat16
HIGHEST = lax.Precision.HIGHEST
FIRST = (((0,), (0,)), ((), ()))
LAST = (((1,), (1,)), ((), ()))
MESH = pl.DeviceIdType.MESH


def step(
    dps,
    vols,
    spots,
    index,
    volume,
    image,
    contrast,
    patch_weight,
    position,
    gain,
    project_in,
    project_out,
    head_weight,
    waves,
    sel,
    places,
    errors_out,
    grad_recv,
    value_out,
    head_out,
    slab_buf,
    picked,
    patches,
    pieces,
    head_wide,
    terms_buf,
    lines,
    patch_buf,
    weight,
    normed,
    attention,
    triple,
    column,
    mean_emb,
    mean_att,
    small_send,
    small_recv,
    pulled_buf,
    slope_buf,
    pooled_buf,
    grad_send,
    tile_send,
    tile_recv,
    head_send,
    line_sems,
    patch_sems,
    weight_sems,
    small_sems,
    grad_sems,
    tile_sems,
    head_sems,
    local_sems,
):
    dp = lax.axis_index("dp")
    vol = lax.axis_index("vol")
    count = dps * vols
    me = dp * vols + vol
    head = dp % HEADS
    base = dp - head
    rows = weight.shape[1]
    width = gain.shape[1]
    slab = volume.shape[0]
    load = pltpu.make_async_copy(volume, slab_buf, local_sems.at[2])
    load.start()

    def copy(src, dst, sems, slot_send, slot_recv, to_dp, to_vol):
        return pltpu.make_async_remote_copy(
            src_ref=src,
            dst_ref=dst,
            send_sem=sems.at[0, slot_send],
            recv_sem=sems.at[1, slot_recv],
            device_id=(to_dp, to_vol),
            device_id_type=MESH,
        )

    barrier = pltpu.get_barrier_semaphore()

    def greet(k, c):
        other = (me + k) % count
        pl.semaphore_signal(
            barrier, inc=1, device_id=(other // vols, other % vols), device_id_type=MESH
        )
        return c

    lax.fori_loop(1, count, greet, 0)
    for h in range(HEADS):
        pieces[h] = jnp.concatenate(
            [project_in[:, p * 512 + h * 64 : p * 512 + h * 64 + 64] for p in range(3)]
            + [project_out[:, h * 64 : h * 64 + 64]],
            axis=1,
        )
    cells = lax.broadcasted_iota(jnp.int32, (16, 16, 128), 1)
    spread_lane = lax.broadcasted_iota(jnp.int32, (16, 16, 128), 2)
    cut = jnp.zeros((PATCHES, 128), F32)
    for r in range(PATCH):
        stripe = image[0, pl.ds(r, 16, stride=PATCH), :]
        stripe = jnp.broadcast_to(stripe[:, None, :], (16, 16, 128))
        stripe = jnp.where(spread_lane // PATCH == cells, stripe, 0.0).reshape(PATCHES, 128)
        cut = cut + jnp.dot(stripe.astype(BF16), places[r], preferred_element_type=F32)
    patches[...] = jnp.concatenate([cut[0:128, 0:64], cut[128:256, 0:64]], axis=1).astype(BF16)
    pl.semaphore_wait(barrier, count - 1)

    def patch_copy(k, slot):
        to = base + (head + k) % HEADS
        return copy(patches, patch_buf.at[slot], patch_sems, k, slot, to, vol)

    def weight_copy(k, slot):
        to = (dp + k) % dps
        return copy(pieces.at[to % HEADS], weight.at[slot], weight_sems, k, slot, to, vol)

    def line_copy(k, slot):
        to = (vol + k) % vols
        return copy(picked.at[k], lines.at[slot], line_sems, k, slot, dp, to)

    def each(first, last, body):
        def run(k, c):
            body(k)
            return c

        lax.fori_loop(first, last, run, 0)

    each(1, HEADS, lambda k: patch_copy(k, head).start())
    each(1, dps, lambda k: weight_copy(k, dp).start())
    own = [
        pltpu.make_async_copy(patches, patch_buf.at[head], local_sems.at[0]),
        pltpu.make_async_copy(pieces.at[head], weight.at[dp], local_sems.at[1]),
    ]
    for one in own:
        one.start()

    cosine = waves[0]
    sine = waves[1]
    pixels = image[0]
    first_cos = jnp.dot(cosine, pixels, precision=HIGHEST, preferred_element_type=F32)
    first_sin = jnp.dot(sine, pixels, precision=HIGHEST, preferred_element_type=F32)
    spectrum = jnp.dot(first_cos, waves[2], precision=HIGHEST, preferred_element_type=F32)
    spectrum = spectrum + jnp.dot(
        first_sin, waves[3], precision=HIGHEST, preferred_element_type=F32
    )
    spectrum = spectrum / PIX

    head_wide[...] = jnp.concatenate([head_weight[...], jnp.zeros((width, 124), F32)], axis=1)
    head_t = head_wide[...].T[0:8]

    own[0].wait()

    def embed(k, c):
        j = (head + k) % HEADS

        @pl.when(k > 0)
        def _():
            patch_copy(HEADS - k, j).wait_recv()

        pair = patch_buf[j]
        sums = jnp.zeros((1, width), F32)
        for half in range(2):
            part = slice(half * 128, half * 128 + 128)
            values = jnp.dot(
                pair[:, half * 64 : half * 64 + 64],
                patch_weight[...],
                preferred_element_type=F32,
            )
            values = (values + position[part].astype(F32)).astype(BF16).astype(F32)
            sums = sums + jnp.sum(values, axis=0, keepdims=True)
            center = values - jnp.mean(values, axis=1, keepdims=True)
            scale = lax.rsqrt(jnp.mean(center * center, axis=1, keepdims=True) + EPSILON)
            normed[j, part, :] = (center * scale * gain[...]).astype(BF16)
        mean_emb[pl.ds(j, 1), :] = sums / PATCHES
        return c

    load.wait()

    def render(step_k, c):
        k = step_k + 1
        v = (vol + k) % vols
        turned = jnp.concatenate([index[v], jnp.zeros((4, 128), jnp.int32)], axis=0)
        turned = turned.astype(F32).T.astype(jnp.int32)
        spot_lane = lax.broadcasted_iota(jnp.int32, (128, 256), 1)
        spot_row = lax.broadcasted_iota(jnp.int32, (128, 256), 0)
        for hyp in range(K):
            line = turned[:, hyp : hyp + 1]
            level = (line >> 8) - vol * slab
            target = jnp.where((level >= 0) & (level < slab), line & 15, 1024)
            hot = jnp.where(spot_lane == (spot_row % 16) * 16 + target, 1.0, 0.0).astype(BF16)
            found = []
            for group in range(8):
                tiles = []
                for i in range(16):
                    spot = spots[v, hyp, group * 16 + i]
                    level = jnp.clip((spot >> 8) - vol * slab, 0, slab - 1)
                    tiles.append(slab_buf[level, (spot >> 4) & 15])
                tiles = jnp.concatenate(tiles, axis=0)
                found.append(
                    jnp.dot(
                        hot[group * 16 : group * 16 + 16], tiles, preferred_element_type=F32
                    )
                )
            found = jnp.concatenate(found, axis=0).astype(BF16)
            picked[k, hyp * PIX : (hyp + 1) * PIX, :] = jnp.dot(
                found, sel[...], preferred_element_type=F32
            ).astype(BF16)

        @pl.when(k < vols)
        def _():
            line_copy(k, vol).start()

        return c

    lax.fori_loop(0, vols, render, 0)
    lines[vol] = picked[vols]
    lax.fori_loop(0, HEADS, embed, 0)

    own[1].wait()
    each(1, dps, lambda k: weight_copy(k, (dp + dps - k) % dps).wait_recv())

    out_w = weight[:, :, 192:256].reshape(width, HEAD_DIM).astype(F32)
    mixed = jnp.dot(head_t, out_w, precision=HIGHEST, preferred_element_type=F32)

    def forward(j, c):
        whole = weight[...].reshape(width, 256)
        t = jnp.dot(normed[j], whole, preferred_element_type=F32).astype(BF16)
        triple[j] = t
        scores = (
            lax.dot_general(t[:, 64:128], t[:, 0:64], LAST, preferred_element_type=F32)
            * HEAD_DIM ** (-0.5)
        )
        raised = jnp.exp(scores)
        chosen = (raised / jnp.sum(raised, axis=0, keepdims=True)).astype(BF16)
        attention[j] = chosen
        col = jnp.sum(chosen.astype(F32), axis=1, keepdims=True)
        column[j] = col
        mean_att[pl.ds(j, 1), :] = (
            jnp.sum(col * t[:, 128:192].astype(F32), axis=0, keepdims=True) / PATCHES
        )
        return c

    lax.fori_loop(0, HEADS, forward, 0)

    each(1, vols, lambda k: line_copy(k, (vol + vols - k) % vols).wait_recv())
    rendered = lines[0].astype(F32)
    for other in range(1, vols):
        rendered = rendered + lines[other].astype(F32)
    slices = rendered
    lane = lax.broadcasted_iota(jnp.int32, (HEADS, 128), 1)
    row = lax.broadcasted_iota(jnp.int32, (HEADS, 128), 0)
    filt = contrast[0].astype(F32)
    misfits = jnp.zeros((HEADS, 128), F32)
    for k in range(K):
        misfit = filt * slices[k * PIX : (k + 1) * PIX] - spectrum
        value = jnp.sum(jnp.sum(misfit * misfit, axis=0, keepdims=True), axis=1, keepdims=True)
        misfits = jnp.where(lane == k, value / (PIX * PIX), misfits)
    errors_out[...] = misfits
    mine = row == head
    own_emb = jnp.where(
        lax.broadcasted_iota(jnp.int32, (HEADS, width), 0) == head, mean_emb[...], 0.0
    )
    logit = lax.dot_general(
        own_emb, head_t, LAST, precision=HIGHEST, preferred_element_type=F32
    )
    logit = logit + lax.dot_general(
        mean_att[...], mixed, LAST, precision=HIGHEST, preferred_element_type=F32
    )
    small_send[0:8, :] = jnp.concatenate([logit, jnp.zeros((HEADS, 120), F32)], axis=1)
    small_send[8:16, :] = jnp.where(mine, misfits, 0.0)

    def small_copy(k, slot):
        to = base + (head + k) % HEADS
        return copy(small_send, small_recv.at[slot], small_sems, k, slot, to, vol)

    each(1, HEADS, lambda k: small_copy(k, head).start())
    small_recv[head] = small_send[...]
    each(1, HEADS, lambda k: small_copy(k, (head + HEADS - k) % HEADS).wait_recv())
    summed = jnp.sum(small_recv[...], axis=0)
    misfits = summed[8:16]
    raised = jnp.where(lane < K, jnp.exp(summed[0:8]), 0.0)
    chances = raised / jnp.sum(raised, axis=1, keepdims=True)
    expected = jnp.sum(chances * misfits, axis=1, keepdims=True)
    slope = chances * (misfits - expected)
    pulled = jnp.zeros((HEADS, HEAD_DIM), F32)
    for k in range(K):
        pulled = pulled + slope[:, k : k + 1] * mixed[k : k + 1, :]
    pulled = pulled / PATCHES

    def backward(j, c):
        t = triple[j]
        chosen = attention[j].astype(F32)
        up = jnp.sum(
            t[:, 128:192].astype(F32) * pulled_buf[pl.ds(j, 1), :], axis=1, keepdims=True
        )
        center = jnp.sum(chosen * up, axis=0, keepdims=True)
        inner = (chosen * (up - center) * HEAD_DIM ** (-0.5)).astype(BF16)
        key_slope = jnp.dot(inner, t[:, 0:64], preferred_element_type=F32)
        query_slope = lax.dot_general(inner, t[:, 64:128], FIRST, preferred_element_type=F32)
        spread = column[j] * slope_buf[pl.ds(j, 1), :]
        terms = jnp.concatenate([query_slope, key_slope, spread], axis=1)
        terms_buf[j] = terms.astype(BF16)
        return c

    pulled_buf[...] = pulled
    slope_buf[...] = slope
    lax.fori_loop(0, HEADS, backward, 0)

    outer = lax.dot_general(
        slope, mean_att[...], FIRST, precision=HIGHEST, preferred_element_type=F32
    )[0:8]
    pooled_t = lax.dot_general(
        jnp.where(mine, slope, 0.0),
        own_emb,
        FIRST,
        precision=HIGHEST,
        preferred_element_type=F32,
    )[0:8]
    pooled_t = pooled_t + lax.dot_general(
        outer, out_w, LAST, precision=HIGHEST, preferred_element_type=F32
    )
    pooled_buf[...] = pooled_t

    chunk = 256 // rows
    chunks = dps // chunk

    def send(d, v, start):
        k = (d * vols + v + count - me) % count
        one = pltpu.make_async_remote_copy(
            src_ref=grad_send.at[d],
            dst_ref=grad_recv.at[me],
            send_sem=grad_sems.at[0, k],
            recv_sem=grad_sems.at[1, me],
            device_id=(d, v),
            device_id_type=MESH,
        )
        two = pltpu.make_async_remote_copy(
            src_ref=tile_send.at[d],
            dst_ref=tile_recv.at[me],
            send_sem=tile_sems.at[0, k],
            recv_sem=tile_sems.at[1, me],
            device_id=(d, v),
            device_id_type=MESH,
        )
        if start:
            two.start()
            one.start()
        else:
            two.wait_send()
            one.wait_send()

    def combine(step_k, c):
        at = (dp // chunk + chunks // 2 + step_k) % chunks
        lanes = pl.ds(pl.multiple_of(at * 256, 256), 256)
        total = lax.dot_general(
            terms_buf[...].reshape(HEADS * PATCHES, 256),
            normed[:, :, lanes].reshape(HEADS * PATCHES, 256),
            FIRST,
            preferred_element_type=F32,
        )
        ours = total[0:128].T.astype(BF16)
        value_t = total[128:136]
        pooled_part = pooled_buf[:, lanes]
        for i in range(chunk):
            part = slice(i * rows, (i + 1) * rows)
            d = at * chunk + i
            grad_send[d] = ours[part]
            fill = [jnp.zeros((HEADS, 64 - rows), F32)] if rows < 64 else []
            top = jnp.concatenate([value_t[:, part]] + fill + [outer], axis=1)
            low = jnp.concatenate([mixed, pooled_part[:, part]] + fill, axis=1)
            tile_send[d] = jnp.where(row < 4, top, pltpu.roll(low, 4, 0))

        def out(n, c2):
            d = at * chunk + n // vols
            v = n % vols

            @pl.when(d * vols + v != me)
            def _():
                send(d, v, True)

            return c2

        lax.fori_loop(0, chunk * vols, out, 0)
        return c

    lax.fori_loop(0, chunks, combine, 0)
    grad_recv[me] = grad_send[dp]
    tile_recv[me] = tile_send[dp]

    def arrived(k, src, dst, sems):
        slot = (me + count - k) % count
        pltpu.make_async_remote_copy(
            src_ref=src.at[dp],
            dst_ref=dst.at[slot],
            send_sem=sems.at[0, k],
            recv_sem=sems.at[1, slot],
            device_id=(dp, vol),
            device_id_type=MESH,
        ).wait_recv()

    each(1, count, lambda k: arrived(k, tile_send, tile_recv, tile_sems))

    pooled_sum = pltpu.roll(jnp.sum(tile_recv[...], axis=0), 4, 0)
    head_send[...] = pooled_sum

    def head_copy(k, slot):
        to = (dp + k) % dps
        return copy(head_send, head_out.at[slot], head_sems, k, slot, to, vol)

    each(1, dps, lambda k: head_copy(k, dp).start())
    head_out[dp] = pooled_sum

    head_own = head_wide[pl.ds(pl.multiple_of(dp * rows, rows), rows), 0:8]
    for h in range(HEADS):
        senders = [(d * vols + v) for d in range(h, dps, HEADS) for v in range(vols)]
        tile = tile_recv[senders[0]]
        mixed_h = jnp.where(row < 4, pltpu.roll(tile, 4, 0), 0.0)[:, 0:64]
        for s in senders[1:]:
            tile = tile + tile_recv[s]
        tile = jnp.where(row < 4, tile, 0.0)
        value_out[:, h * 64 : h * 64 + 64] = (
            lax.dot_general(
                tile[:, 0:rows], mixed_h, FIRST, precision=HIGHEST, preferred_element_type=F32
            )
            / PATCHES
        )
        value_out[:, 512 + h * 64 : 576 + h * 64] = jnp.dot(
            head_own, tile[:, 64:128], precision=HIGHEST, preferred_element_type=F32
        )
    each(1, count, lambda k: arrived(k, grad_send, grad_recv, grad_sems))
    each(1, dps, lambda k: head_copy(k, (dp + dps - k) % dps).wait_recv())

    each(1, HEADS, lambda k: patch_copy(k, head).wait_send())
    each(1, dps, lambda k: weight_copy(k, dp).wait_send())
    each(1, vols, lambda k: line_copy(k, vol).wait_send())
    each(1, HEADS, lambda k: small_copy(k, head).wait_send())
    each(1, count, lambda k: send(((me + k) % count) // vols, (me + k) % vols, False))
    each(1, dps, lambda k: head_copy(k, dp).wait_send())


def finish(dps, vols, errors, grads, values, heads, errors_out, in_out, out_out, head_out):
    rows = values.shape[0]
    for h in range(HEADS):
        senders = [(d * vols + v) for d in range(h, dps, HEADS) for v in range(vols)]
        both = grads[senders[0]].astype(F32)
        for s in senders[1:]:
            both = both + grads[s].astype(F32)
        in_out[:, h * 64 : h * 64 + 64] = both[:, 0:64]
        in_out[:, 512 + h * 64 : 576 + h * 64] = both[:, 64:128]
    in_out[:, 1024:1536] = values[:, 0:512]
    out_out[...] = values[:, 512:1024]
    errors_out[...] = errors[0:1, 0:K]
    for d in range(dps):
        head_out[d * rows : (d + 1) * rows, :] = heads[d].T[64 : 64 + rows, 0:K]


def constants():
    freq = np.arange(PIX) - PIX // 2
    phase = (freq[:, None] * np.arange(PIX)[None, :] % PIX) * (2.0 * math.pi / PIX)
    cosine, sine = np.cos(phase), np.sin(phase)
    waves = np.stack([cosine, sine, (cosine + sine).T, (cosine - sine).T]).astype(np.float32)
    sel = np.zeros((2 * PIX, PIX), np.float32)
    sel[2 * np.arange(PIX), np.arange(PIX)] = 1.0
    places = np.zeros((PATCH, PIX, PIX), np.float32)
    for r in range(PATCH):
        places[r, np.arange(PIX), r * PATCH + np.arange(PIX) % PATCH] = 1.0
    return waves, sel, places


def local(
    dps,
    vols,
    images,
    contrast,
    volume,
    line_index,
    patch_weight,
    position,
    norm_gain,
    project_in,
    project_out,
    head_weight,
):
    width = norm_gain.shape[0]
    rows = project_in.shape[0]
    count = dps * vols
    waves, sel, places = constants()
    slab, side, _ = volume.shape
    vmem = pl.BlockSpec(memory_space=pltpu.VMEM)
    errors, grads, values, heads = pl.pallas_call(
        functools.partial(step, dps, vols),
        out_shape=(
            jax.ShapeDtypeStruct((8, 128), F32),
            jax.ShapeDtypeStruct((count, rows, 128), BF16),
            jax.ShapeDtypeStruct((rows, 1024), F32),
            jax.ShapeDtypeStruct((dps, 8, 128), F32),
        ),
        in_specs=[
            pl.BlockSpec(memory_space=pltpu.SMEM),
            vmem,
            pl.BlockSpec(memory_space=pltpu.HBM),
        ]
        + [vmem] * 11,
        out_specs=(vmem,) * 4,
        scratch_shapes=[
            pltpu.VMEM((slab, 16, 16, side), BF16),
            pltpu.VMEM((vols + 1, K * PIX, PIX), BF16),
            pltpu.VMEM((PATCHES // 2, 128), BF16),
            pltpu.VMEM((HEADS, rows, 256), BF16),
            pltpu.VMEM((width, 128), F32),
            pltpu.VMEM((HEADS, PATCHES, 256), BF16),
            pltpu.VMEM((vols, K * PIX, PIX), BF16),
            pltpu.VMEM((HEADS, PATCHES // 2, 128), BF16),
            pltpu.VMEM((dps, rows, 256), BF16),
            pltpu.VMEM((HEADS, PATCHES, width), BF16),
            pltpu.VMEM((HEADS, PATCHES, PATCHES), BF16),
            pltpu.VMEM((HEADS, PATCHES, 256), BF16),
            pltpu.VMEM((HEADS, PATCHES, 1), F32),
            pltpu.VMEM((HEADS, width), F32),
            pltpu.VMEM((HEADS, HEAD_DIM), F32),
            pltpu.VMEM((16, 128), F32),
            pltpu.VMEM((HEADS, 16, 128), F32),
            pltpu.VMEM((HEADS, HEAD_DIM), F32),
            pltpu.VMEM((HEADS, 128), F32),
            pltpu.VMEM((HEADS, width), F32),
            pltpu.VMEM((dps, rows, 128), BF16),
            pltpu.VMEM((dps, 8, 128), F32),
            pltpu.VMEM((count, 8, 128), F32),
            pltpu.VMEM((8, 128), F32),
            pltpu.SemaphoreType.DMA((2, vols)),
            pltpu.SemaphoreType.DMA((2, HEADS)),
            pltpu.SemaphoreType.DMA((2, dps)),
            pltpu.SemaphoreType.DMA((2, HEADS)),
            pltpu.SemaphoreType.DMA((2, count)),
            pltpu.SemaphoreType.DMA((2, count)),
            pltpu.SemaphoreType.DMA((2, dps)),
            pltpu.SemaphoreType.DMA((3,)),
        ],
        compiler_params=pltpu.CompilerParams(
            collective_id=0, has_side_effects=True, vmem_limit_bytes=56 * 1024 * 1024
        ),
        name="pose_step",
    )(
        line_index,
        line_index,
        volume.reshape(slab, side // 16, 16, side),
        images,
        contrast,
        patch_weight,
        position,
        norm_gain.reshape(1, width),
        project_in,
        project_out,
        head_weight,
        jnp.asarray(waves),
        jnp.asarray(sel, BF16),
        jnp.asarray(places, BF16),
    )
    return pl.pallas_call(
        functools.partial(finish, dps, vols),
        out_shape=(
            jax.ShapeDtypeStruct((1, K), F32),
            jax.ShapeDtypeStruct((rows, 3 * HEADS * HEAD_DIM), F32),
            jax.ShapeDtypeStruct((rows, HEADS * HEAD_DIM), F32),
            jax.ShapeDtypeStruct((width, K), F32),
        ),
        in_specs=[vmem] * 4,
        out_specs=(vmem,) * 4,
        name="finish",
    )(errors, grads, values, heads)


def solution(mesh):
    placed = (
        P(("dp", "vol"), None, None),
        P(("dp", "vol"), None, None),
        P("vol", None, None),
        P("dp", None, None),
        P(),
        P(),
        P(),
        P("dp", None),
        P("dp", None),
        P(),
    )
    return jax.shard_map(
        functools.partial(local, mesh.shape["dp"], mesh.shape["vol"]),
        mesh=mesh,
        in_specs=placed,
        out_specs=(P(("dp", "vol"), None), P("dp", None), P("dp", None), P()),
        check_vma=False,
    )
```

```python
import functools
import math

import jax
import jax.numpy as jnp
import numpy as np
from jax import lax
from jax.experimental import pallas as pl
from jax.experimental.pallas import tpu as pltpu
from jax.sharding import PartitionSpec as P

HEADS = 8
HEAD_DIM = 64
PIX = 128
PATCH = 8
PATCHES = 256
K = 4
EPSILON = 1e-05
F32 = jnp.float32
BF16 = jnp.bfloat16
HIGHEST = lax.Precision.HIGHEST
FIRST = (((0,), (0,)), ((), ()))
LAST = (((1,), (1,)), ((), ()))
MESH = pl.DeviceIdType.MESH


def step(
    dps,
    vols,
    spots,
    index,
    volume,
    image,
    contrast,
    patch_weight,
    position,
    gain,
    project_in,
    project_out,
    head_weight,
    waves,
    sel,
    places,
    errors_out,
    grad_recv,
    value_out,
    head_out,
    slab_buf,
    picked,
    patches,
    pieces,
    head_wide,
    terms_buf,
    lines,
    patch_buf,
    weight,
    normed,
    attention,
    triple,
    column,
    mean_emb,
    mean_att,
    small_send,
    small_recv,
    pulled_buf,
    slope_buf,
    pooled_buf,
    grad_send,
    tile_send,
    tile_recv,
    head_send,
    line_sems,
    patch_sems,
    weight_sems,
    small_sems,
    grad_sems,
    tile_sems,
    head_sems,
    local_sems,
    relay_sems,
    pass_sems,
):
    dp = lax.axis_index("dp")
    vol = lax.axis_index("vol")
    count = dps * vols
    me = dp * vols + vol
    head = dp % HEADS
    base = dp - head
    rows = weight.shape[1]
    width = gain.shape[1]
    slab = volume.shape[0]
    load = pltpu.make_async_copy(volume, slab_buf, local_sems.at[2])
    load.start()

    def copy(src, dst, sems, slot_send, slot_recv, to_dp, to_vol):
        return pltpu.make_async_remote_copy(
            src_ref=src,
            dst_ref=dst,
            send_sem=sems.at[0, slot_send],
            recv_sem=sems.at[1, slot_recv],
            device_id=(to_dp, to_vol),
            device_id_type=MESH,
        )

    barrier = pltpu.get_barrier_semaphore()

    def greet(k, c):
        other = (me + k) % count
        pl.semaphore_signal(
            barrier, inc=1, device_id=(other // vols, other % vols), device_id_type=MESH
        )
        return c

    lax.fori_loop(1, count, greet, 0)
    for h in range(HEADS):
        pieces[h] = jnp.concatenate(
            [project_in[:, p * 512 + h * 64 : p * 512 + h * 64 + 64] for p in range(3)]
            + [project_out[:, h * 64 : h * 64 + 64]],
            axis=1,
        )
    cells = lax.broadcasted_iota(jnp.int32, (16, 16, 128), 1)
    spread_lane = lax.broadcasted_iota(jnp.int32, (16, 16, 128), 2)
    cut = jnp.zeros((PATCHES, 128), F32)
    for r in range(PATCH):
        stripe = image[0, pl.ds(r, 16, stride=PATCH), :]
        stripe = jnp.broadcast_to(stripe[:, None, :], (16, 16, 128))
        stripe = jnp.where(spread_lane // PATCH == cells, stripe, 0.0).reshape(PATCHES, 128)
        cut = cut + jnp.dot(stripe.astype(BF16), places[r], preferred_element_type=F32)
    patches[...] = jnp.concatenate([cut[0:128, 0:64], cut[128:256, 0:64]], axis=1).astype(BF16)
    pl.semaphore_wait(barrier, count - 1)

    def patch_copy(k, slot):
        to = base + (head + k) % HEADS
        return copy(patches, patch_buf.at[slot], patch_sems, k, slot, to, vol)

    def weight_copy(k, slot):
        to = (dp + k) % dps
        return copy(pieces.at[to % HEADS], weight.at[slot], weight_sems, k, slot, to, vol)

    def line_copy(k, slot):
        to = (vol + k) % vols
        return copy(picked.at[k], lines.at[slot], line_sems, k, slot, dp, to)

    def each(first, last, body):
        def run(k, c):
            body(k)
            return c

        lax.fori_loop(first, last, run, 0)

    each(1, HEADS, lambda k: patch_copy(k, head).start())
    share = dp % vols == vol

    def weight_start(k, start):
        to = (dp + k) % dps

        @pl.when(jnp.logical_or(to // HEADS == dp // HEADS, share))
        def _():
            if start:
                weight_copy(k, dp).start()
            else:
                weight_copy(k, dp).wait_send()

    each(1, dps, lambda k: weight_start(dps - k, True))

    def weight_relay(n, v_step):
        s = (base + HEADS + n) % dps
        return pltpu.make_async_remote_copy(
            src_ref=weight.at[s],
            dst_ref=weight.at[s],
            send_sem=pass_sems.at[n * vols + v_step],
            recv_sem=weight_sems.at[1, s],
            device_id=(dp, (vol + v_step) % vols),
            device_id_type=MESH,
        )

    def weight_pass(n, start):
        s = (base + HEADS + n) % dps

        @pl.when(s % vols == vol)
        def _():
            if start:
                weight_copy((dp + dps - s) % dps, s).wait_recv()
                each(1, vols, lambda v_step: weight_relay(n, v_step).start())
            else:
                each(1, vols, lambda v_step: weight_relay(n, v_step).wait_send())

    def weight_rest(k):
        s = (dp + dps - k) % dps

        @pl.when(jnp.logical_or(s // HEADS == dp // HEADS, s % vols != vol))
        def _():
            weight_copy(k, s).wait_recv()

    own = [
        pltpu.make_async_copy(patches, patch_buf.at[head], local_sems.at[0]),
        pltpu.make_async_copy(pieces.at[head], weight.at[dp], local_sems.at[1]),
    ]
    for one in own:
        one.start()

    cosine = waves[0]
    sine = waves[1]
    pixels = image[0]
    first_cos = jnp.dot(cosine, pixels, precision=HIGHEST, preferred_element_type=F32)
    first_sin = jnp.dot(sine, pixels, precision=HIGHEST, preferred_element_type=F32)
    spectrum = jnp.dot(first_cos, waves[2], precision=HIGHEST, preferred_element_type=F32)
    spectrum = spectrum + jnp.dot(
        first_sin, waves[3], precision=HIGHEST, preferred_element_type=F32
    )
    spectrum = spectrum / PIX

    head_t = jnp.concatenate([head_weight[...], jnp.zeros((4, width), F32)], axis=0)
    near = pl.ds(pl.multiple_of(dp * rows // 128 * 128, 128), 128)
    head_wide[...] = jnp.concatenate(
        [head_weight[:, near], jnp.zeros((4, 128), F32)], axis=0
    ).T

    own[0].wait()

    def embed(k, c):
        j = (head + k) % HEADS

        @pl.when(k > 0)
        def _():
            patch_copy(HEADS - k, j).wait_recv()

        pair = patch_buf[j]
        sums = jnp.zeros((1, width), F32)
        for half in range(2):
            part = slice(half * 128, half * 128 + 128)
            values = jnp.dot(
                pair[:, half * 64 : half * 64 + 64],
                patch_weight[...],
                preferred_element_type=F32,
            )
            values = (values + position[part].astype(F32)).astype(BF16).astype(F32)
            sums = sums + jnp.sum(values, axis=0, keepdims=True)
            center = values - jnp.mean(values, axis=1, keepdims=True)
            scale = lax.rsqrt(jnp.mean(center * center, axis=1, keepdims=True) + EPSILON)
            normed[j, part, :] = (center * scale * gain[...]).astype(BF16)
        mean_emb[pl.ds(j, 1), :] = sums / PATCHES
        return c

    load.wait()

    def render(step_k, c):
        k = step_k + 1
        v = (vol + k) % vols
        turned = jnp.concatenate([index[v], jnp.zeros((4, 128), jnp.int32)], axis=0)
        turned = turned.astype(F32).T.astype(jnp.int32)
        spot_lane = lax.broadcasted_iota(jnp.int32, (128, 256), 1)
        spot_row = lax.broadcasted_iota(jnp.int32, (128, 256), 0)
        for hyp in range(K):
            line = turned[:, hyp : hyp + 1]
            level = (line >> 8) - vol * slab
            target = jnp.where((level >= 0) & (level < slab), line & 15, 1024)
            hot = jnp.where(spot_lane == (spot_row % 16) * 16 + target, 1.0, 0.0).astype(BF16)
            found = []
            for group in range(8):
                tiles = []
                for i in range(16):
                    spot = spots[v, hyp, group * 16 + i]
                    level = jnp.clip((spot >> 8) - vol * slab, 0, slab - 1)
                    tiles.append(slab_buf[level, (spot >> 4) & 15])
                tiles = jnp.concatenate(tiles, axis=0)
                found.append(
                    jnp.dot(
                        hot[group * 16 : group * 16 + 16], tiles, preferred_element_type=F32
                    )
                )
            found = jnp.concatenate(found, axis=0).astype(BF16)
            picked[k, hyp * PIX : (hyp + 1) * PIX, :] = jnp.dot(
                found, sel[...], preferred_element_type=F32
            ).astype(BF16)

        @pl.when(k < vols)
        def _():
            line_copy(k, vol).start()

        return c

    lax.fori_loop(0, vols, render, 0)
    lines[vol] = picked[vols]
    lax.fori_loop(0, 4, embed, 0)
    each(0, dps - HEADS, lambda n: weight_pass(n, True))
    lax.fori_loop(4, HEADS, embed, 0)

    own[1].wait()
    each(1, dps, weight_rest)

    out_w = weight[:, :, 192:256].reshape(width, HEAD_DIM).astype(F32)
    mixed = jnp.dot(head_t, out_w, precision=HIGHEST, preferred_element_type=F32)

    def forward(j, c):
        whole = weight[...].reshape(width, 256)
        t = jnp.dot(normed[j], whole, preferred_element_type=F32).astype(BF16)
        triple[j] = t
        scores = (
            lax.dot_general(t[:, 64:128], t[:, 0:64], LAST, preferred_element_type=F32)
            * HEAD_DIM ** (-0.5)
        )
        raised = jnp.exp(scores)
        chosen = (raised / jnp.sum(raised, axis=0, keepdims=True)).astype(BF16)
        attention[j] = chosen
        col = jnp.sum(chosen.astype(F32), axis=1, keepdims=True)
        column[j] = col
        mean_att[pl.ds(j, 1), :] = (
            jnp.sum(col * t[:, 128:192].astype(F32), axis=0, keepdims=True) / PATCHES
        )
        return c

    lax.fori_loop(0, HEADS, forward, 0)

    each(1, vols, lambda k: line_copy(k, (vol + vols - k) % vols).wait_recv())
    rendered = lines[0].astype(F32)
    for other in range(1, vols):
        rendered = rendered + lines[other].astype(F32)
    slices = rendered
    lane = lax.broadcasted_iota(jnp.int32, (HEADS, 128), 1)
    row = lax.broadcasted_iota(jnp.int32, (HEADS, 128), 0)
    filt = contrast[0].astype(F32)
    misfits = jnp.zeros((HEADS, 128), F32)
    for k in range(K):
        misfit = filt * slices[k * PIX : (k + 1) * PIX] - spectrum
        value = jnp.sum(jnp.sum(misfit * misfit, axis=0, keepdims=True), axis=1, keepdims=True)
        misfits = jnp.where(lane == k, value / (PIX * PIX), misfits)
    errors_out[...] = misfits
    mine = row == head
    own_emb = jnp.where(
        lax.broadcasted_iota(jnp.int32, (HEADS, width), 0) == head, mean_emb[...], 0.0
    )
    logit = lax.dot_general(
        own_emb, head_t, LAST, precision=HIGHEST, preferred_element_type=F32
    )
    logit = logit + lax.dot_general(
        mean_att[...], mixed, LAST, precision=HIGHEST, preferred_element_type=F32
    )
    small_send[0:8, :] = jnp.concatenate([logit, jnp.zeros((HEADS, 120), F32)], axis=1)
    small_send[8:16, :] = jnp.where(mine, misfits, 0.0)

    def small_copy(k, slot):
        to = base + (head + k) % HEADS
        return copy(small_send, small_recv.at[slot], small_sems, k, slot, to, vol)

    each(1, HEADS, lambda k: small_copy(k, head).start())
    small_recv[head] = small_send[...]
    each(1, HEADS, lambda k: small_copy(k, (head + HEADS - k) % HEADS).wait_recv())
    summed = jnp.sum(small_recv[...], axis=0)
    misfits = summed[8:16]
    raised = jnp.where(lane < K, jnp.exp(summed[0:8]), 0.0)
    chances = raised / jnp.sum(raised, axis=1, keepdims=True)
    expected = jnp.sum(chances * misfits, axis=1, keepdims=True)
    slope = chances * (misfits - expected)
    pulled = jnp.zeros((HEADS, HEAD_DIM), F32)
    for k in range(K):
        pulled = pulled + slope[:, k : k + 1] * mixed[k : k + 1, :]
    pulled = pulled / PATCHES

    def backward(j, c):
        t = triple[j]
        chosen = attention[j].astype(F32)
        up = jnp.sum(
            t[:, 128:192].astype(F32) * pulled_buf[pl.ds(j, 1), :], axis=1, keepdims=True
        )
        center = jnp.sum(chosen * up, axis=0, keepdims=True)
        inner = (chosen * (up - center) * HEAD_DIM ** (-0.5)).astype(BF16)
        key_slope = jnp.dot(inner, t[:, 0:64], preferred_element_type=F32)
        query_slope = lax.dot_general(inner, t[:, 64:128], FIRST, preferred_element_type=F32)
        spread = column[j] * slope_buf[pl.ds(j, 1), :]
        terms = jnp.concatenate([query_slope, key_slope, spread], axis=1)
        terms_buf[j] = terms.astype(BF16)
        return c

    pulled_buf[...] = pulled
    slope_buf[...] = slope
    lax.fori_loop(0, HEADS, backward, 0)

    outer = lax.dot_general(
        slope, mean_att[...], FIRST, precision=HIGHEST, preferred_element_type=F32
    )[0:8]
    pooled_t = lax.dot_general(
        jnp.where(mine, slope, 0.0),
        own_emb,
        FIRST,
        precision=HIGHEST,
        preferred_element_type=F32,
    )[0:8]
    pooled_t = pooled_t + lax.dot_general(
        outer, out_w, LAST, precision=HIGHEST, preferred_element_type=F32
    )
    pooled_buf[...] = pooled_t

    chunk = 256 // rows
    chunks = dps // chunk

    def send(d, v, start):
        k = (d * vols + v + count - me) % count
        one = pltpu.make_async_remote_copy(
            src_ref=grad_send.at[d],
            dst_ref=grad_recv.at[me],
            send_sem=grad_sems.at[0, k],
            recv_sem=grad_sems.at[1, me],
            device_id=(d, v),
            device_id_type=MESH,
        )
        two = pltpu.make_async_remote_copy(
            src_ref=tile_send.at[d],
            dst_ref=tile_recv.at[me],
            send_sem=tile_sems.at[0, k],
            recv_sem=tile_sems.at[1, me],
            device_id=(d, v),
            device_id_type=MESH,
        )
        near = jnp.logical_or(d // HEADS == dp // HEADS, v == vol)
        if start:
            two.start()
        else:
            two.wait_send()

        @pl.when(near)
        def _():
            if start:
                one.start()
            else:
                one.wait_send()

    def combine(step_k, c):
        at = (dp // chunk + chunks // 2 + step_k) % chunks
        lanes = pl.ds(pl.multiple_of(at * 256, 256), 256)
        total = lax.dot_general(
            terms_buf[...].reshape(HEADS * PATCHES, 256),
            normed[:, :, lanes].reshape(HEADS * PATCHES, 256),
            FIRST,
            preferred_element_type=F32,
        )
        ours = total[0:128].T.astype(BF16)
        value_t = total[128:136]
        pooled_part = pooled_buf[:, lanes]
        for i in range(chunk):
            part = slice(i * rows, (i + 1) * rows)
            d = at * chunk + i
            grad_send[d] = ours[part]
            fill = [jnp.zeros((HEADS, 64 - rows), F32)] if rows < 64 else []
            top = jnp.concatenate([value_t[:, part]] + fill + [outer], axis=1)
            low = jnp.concatenate([mixed, pooled_part[:, part]] + fill, axis=1)
            tile_send[d] = jnp.where(row < 4, top, pltpu.roll(low, 4, 0))

        def out(n, c2):
            d = at * chunk + n // vols
            v = n % vols

            @pl.when(d * vols + v != me)
            def _():
                send(d, v, True)

            return c2

        lax.fori_loop(0, chunk * vols, out, 0)
        return c

    lax.fori_loop(0, chunks, combine, 0)
    grad_recv[me] = grad_send[dp]
    tile_recv[me] = tile_send[dp]

    def arrived(k, src, dst, sems):
        slot = (me + count - k) % count
        pltpu.make_async_remote_copy(
            src_ref=src.at[dp],
            dst_ref=dst.at[slot],
            send_sem=sems.at[0, k],
            recv_sem=sems.at[1, slot],
            device_id=(dp, vol),
            device_id_type=MESH,
        ).wait_recv()

    each(1, count, lambda k: arrived(k, tile_send, tile_recv, tile_sems))

    pooled_sum = pltpu.roll(jnp.sum(tile_recv[...], axis=0), 4, 0)
    head_send[...] = pooled_sum

    def head_copy(k, slot):
        to = (dp + k) % dps
        return copy(head_send, head_out.at[slot], head_sems, k, slot, to, vol)

    each(1, dps, lambda k: head_copy(k, dp).start())
    head_out[dp] = pooled_sum

    head_own = head_wide[pl.ds(pl.multiple_of(dp * rows % 128, rows), rows), :]
    for h in range(HEADS):
        senders = [(d * vols + v) for d in range(h, dps, HEADS) for v in range(vols)]
        tile = tile_recv[senders[0]]
        mixed_h = jnp.where(row < 4, pltpu.roll(tile, 4, 0), 0.0)[:, 0:64]
        for s in senders[1:]:
            tile = tile + tile_recv[s]
        tile = jnp.where(row < 4, tile, 0.0)
        value_out[:, h * 64 : h * 64 + 64] = (
            lax.dot_general(
                tile[:, 0:rows], mixed_h, FIRST, precision=HIGHEST, preferred_element_type=F32
            )
            / PATCHES
        )
        value_out[:, 512 + h * 64 : 576 + h * 64] = jnp.dot(
            head_own, tile[:, 64:128], precision=HIGHEST, preferred_element_type=F32
        )

    far = dps - HEADS

    def relay(n, v_step):
        s = (base + HEADS + n) % dps
        slot = s * vols + vol
        return pltpu.make_async_remote_copy(
            src_ref=grad_recv.at[slot],
            dst_ref=grad_recv.at[slot],
            send_sem=relay_sems.at[n * vols + v_step],
            recv_sem=grad_sems.at[1, slot],
            device_id=(dp, (vol + v_step) % vols),
            device_id_type=MESH,
        )

    def pass_on(n):
        slot = ((base + HEADS + n) % dps) * vols + vol
        arrived((me + count - slot) % count, grad_send, grad_recv, grad_sems)
        each(1, vols, lambda v_step: relay(n, v_step).start())

    each(0, far, pass_on)

    def rest(k):
        slot = (me + count - k) % count

        @pl.when(jnp.logical_or(slot // vols // HEADS == dp // HEADS, slot % vols != vol))
        def _():
            arrived(k, grad_send, grad_recv, grad_sems)

    each(1, count, rest)
    each(0, far, lambda n: each(1, vols, lambda v_step: relay(n, v_step).wait_send()))
    each(1, dps, lambda k: head_copy(k, (dp + dps - k) % dps).wait_recv())

    each(1, HEADS, lambda k: patch_copy(k, head).wait_send())
    each(1, dps, lambda k: weight_start(dps - k, False))
    each(0, dps - HEADS, lambda n: weight_pass(n, False))
    each(1, vols, lambda k: line_copy(k, vol).wait_send())
    each(1, HEADS, lambda k: small_copy(k, head).wait_send())
    each(1, count, lambda k: send(((me + k) % count) // vols, (me + k) % vols, False))
    each(1, dps, lambda k: head_copy(k, dp).wait_send())


def finish(dps, vols, errors, grads, values, heads, errors_out, in_out, out_out, head_out):
    rows = values.shape[0]
    for h in range(HEADS):
        senders = [(d * vols + v) for d in range(h, dps, HEADS) for v in range(vols)]
        both = grads[senders[0]].astype(F32)
        for s in senders[1:]:
            both = both + grads[s].astype(F32)
        in_out[:, h * 64 : h * 64 + 64] = both[:, 0:64]
        in_out[:, 512 + h * 64 : 576 + h * 64] = both[:, 64:128]
    in_out[:, 1024:1536] = values[:, 0:512]
    out_out[...] = values[:, 512:1024]
    errors_out[...] = errors[0:1, 0:K]
    for d in range(dps):
        head_out[:, d * rows : (d + 1) * rows] = heads[d][0:K, 64 : 64 + rows]


def constants():
    freq = np.arange(PIX) - PIX // 2
    phase = (freq[:, None] * np.arange(PIX)[None, :] % PIX) * (2.0 * math.pi / PIX)
    cosine, sine = np.cos(phase), np.sin(phase)
    waves = np.stack([cosine, sine, (cosine + sine).T, (cosine - sine).T]).astype(np.float32)
    sel = np.zeros((2 * PIX, PIX), np.float32)
    sel[2 * np.arange(PIX), np.arange(PIX)] = 1.0
    places = np.zeros((PATCH, PIX, PIX), np.float32)
    for r in range(PATCH):
        places[r, np.arange(PIX), r * PATCH + np.arange(PIX) % PATCH] = 1.0
    return waves, sel, places


def local(
    dps,
    vols,
    images,
    contrast,
    volume,
    line_index,
    patch_weight,
    position,
    norm_gain,
    project_in,
    project_out,
    head_weight,
):
    width = norm_gain.shape[0]
    rows = project_in.shape[0]
    count = dps * vols
    waves, sel, places = constants()
    slab, side, _ = volume.shape
    vmem = pl.BlockSpec(memory_space=pltpu.VMEM)
    errors, grads, values, heads = pl.pallas_call(
        functools.partial(step, dps, vols),
        out_shape=(
            jax.ShapeDtypeStruct((8, 128), F32),
            jax.ShapeDtypeStruct((count, rows, 128), BF16),
            jax.ShapeDtypeStruct((rows, 1024), F32),
            jax.ShapeDtypeStruct((dps, 8, 128), F32),
        ),
        in_specs=[
            pl.BlockSpec(memory_space=pltpu.SMEM),
            vmem,
            pl.BlockSpec(memory_space=pltpu.HBM),
        ]
        + [vmem] * 11,
        out_specs=(vmem,) * 4,
        scratch_shapes=[
            pltpu.VMEM((slab, 16, 16, side), BF16),
            pltpu.VMEM((vols + 1, K * PIX, PIX), BF16),
            pltpu.VMEM((PATCHES // 2, 128), BF16),
            pltpu.VMEM((HEADS, rows, 256), BF16),
            pltpu.VMEM((128, 8), F32),
            pltpu.VMEM((HEADS, PATCHES, 256), BF16),
            pltpu.VMEM((vols, K * PIX, PIX), BF16),
            pltpu.VMEM((HEADS, PATCHES // 2, 128), BF16),
            pltpu.VMEM((dps, rows, 256), BF16),
            pltpu.VMEM((HEADS, PATCHES, width), BF16),
            pltpu.VMEM((HEADS, PATCHES, PATCHES), BF16),
            pltpu.VMEM((HEADS, PATCHES, 256), BF16),
            pltpu.VMEM((HEADS, PATCHES, 1), F32),
            pltpu.VMEM((HEADS, width), F32),
            pltpu.VMEM((HEADS, HEAD_DIM), F32),
            pltpu.VMEM((16, 128), F32),
            pltpu.VMEM((HEADS, 16, 128), F32),
            pltpu.VMEM((HEADS, HEAD_DIM), F32),
            pltpu.VMEM((HEADS, 128), F32),
            pltpu.VMEM((HEADS, width), F32),
            pltpu.VMEM((dps, rows, 128), BF16),
            pltpu.VMEM((dps, 8, 128), F32),
            pltpu.VMEM((count, 8, 128), F32),
            pltpu.VMEM((8, 128), F32),
            pltpu.SemaphoreType.DMA((2, vols)),
            pltpu.SemaphoreType.DMA((2, HEADS)),
            pltpu.SemaphoreType.DMA((2, dps)),
            pltpu.SemaphoreType.DMA((2, HEADS)),
            pltpu.SemaphoreType.DMA((2, count)),
            pltpu.SemaphoreType.DMA((2, count)),
            pltpu.SemaphoreType.DMA((2, dps)),
            pltpu.SemaphoreType.DMA((3,)),
            pltpu.SemaphoreType.DMA((dps * vols,)),
            pltpu.SemaphoreType.DMA((dps * vols,)),
        ],
        compiler_params=pltpu.CompilerParams(
            collective_id=0, has_side_effects=True, vmem_limit_bytes=56 * 1024 * 1024
        ),
        name="pose_step",
    )(
        line_index,
        line_index,
        volume.reshape(slab, side // 16, 16, side),
        images,
        contrast,
        patch_weight,
        position,
        norm_gain.reshape(1, width),
        project_in,
        project_out,
        head_weight.T,
        jnp.asarray(waves),
        jnp.asarray(sel, BF16),
        jnp.asarray(places, BF16),
    )
    errors, in_grad, out_grad, head_grad = pl.pallas_call(
        functools.partial(finish, dps, vols),
        out_shape=(
            jax.ShapeDtypeStruct((1, K), F32),
            jax.ShapeDtypeStruct((rows, 3 * HEADS * HEAD_DIM), F32),
            jax.ShapeDtypeStruct((rows, HEADS * HEAD_DIM), F32),
            jax.ShapeDtypeStruct((K, width), F32),
        ),
        in_specs=[vmem] * 4,
        out_specs=(vmem,) * 4,
        name="finish",
    )(errors, grads, values, heads)
    return errors, in_grad, out_grad, head_grad.T


def solution(mesh):
    placed = (
        P(("dp", "vol"), None, None),
        P(("dp", "vol"), None, None),
        P("vol", None, None),
        P("dp", None, None),
        P(),
        P(),
        P(),
        P("dp", None),
        P("dp", None),
        P(),
    )
    return jax.shard_map(
        functools.partial(local, mesh.shape["dp"], mesh.shape["vol"]),
        mesh=mesh,
        in_specs=placed,
        out_specs=(P(("dp", "vol"), None), P("dp", None), P("dp", None), P()),
        check_vma=False,
    )
```
